32 devices in a mesh: site: 4 (over y, x), bond: 8 (over z, core).
Axes of the slice: x: 2, y: 2, z: 4, core: 2. Of those that a mesh axis runs over, the one named last changes fastest.
Arguments:
- start_rows: bfloat16 [1024, 4096], P(None, 'bond'), may hold values from -6 to 6
- site_tensors: bfloat16 [4, 4096, 8, 4096], P('site', None, None, 'bond'), may hold values from -0.09375 to 0.09375
- block_scales: float32 [4, 8, 32], P('site', None, 'bond'), may hold values from 0.25 to 1
- displacement: float32 [4, 8, 8], P('site'), may hold values from -0.9 to 0.9
- outcomes: int32 [4, 1024], P('site'), may hold values from 0 to 7
Outputs:
- leaving: bfloat16 [4, 1024, 4096], P('site', None, 'bond')
- log_norms: float32 [4, 1024], P('site')
The draws below stay inside these ranges and needn't reach their ends.
Inputs may be any that keep to these rules, and one draw needn't show every extreme that they name: outcomes index the second dimension of displacement.
All inputs are finite; a program needn't handle non-finite values.
Results may differ from the reference program's by a relative error of at most 0.014.
Values may be sent and summed in bfloat16 or wider, within the bound.
A program may use at most 128 MiB of HBM per device.

```python
import math
import jax
import jax.numpy as jnp
from jax import lax

CHI = 4096
PHYS = 8
BLOCK = 128
SITES = 4
ALLROWS = 1024


def touch_ends(values, own_key, low, high):
    longest = values.shape.index(max(values.shape))
    spots = []
    for shift in (0, 1):
        where = [jax.random.randint(jax.random.fold_in(own_key, axis), (), 0, length) for axis, length in enumerate(values.shape)]
        where[longest] = (where[longest] + shift) % values.shape[longest]
        spots.append(tuple(where))
    return values.at[spots[0]].set(low).at[spots[1]].set(high)


def block_scale(own_key, dims, shards, least, high):
    def one(axis_at, blocks):
        steps = jax.random.uniform(jax.random.fold_in(jax.random.fold_in(own_key, 6), axis_at), (blocks,), jnp.float32, least / len(shards), high / len(shards))
        return jnp.repeat(jnp.exp(steps), dims[axis_at] // blocks).reshape((-1,) + (1,) * (len(dims) - axis_at - 1))

    loudness = one(*shards[0])
    for cut in shards[1:]:
        loudness = loudness * one(*cut)
    return loudness


def gaussian(stream_key, dims, width, most, split=(), held_as=jnp.bfloat16):
    factor_of = block_scale(stream_key, dims, split, -0.22, 0.18) if split else 1.0
    drawn = jax.random.normal(stream_key, dims, jnp.float32) * width * factor_of
    return jnp.minimum(jnp.maximum(drawn, -most), most).astype(held_as)


def setup_inputs(seed: int = 0) -> dict:
    key_of = jax.random.split(jax.random.key(seed), 6)
    return {
        "start_rows": gaussian(key_of[0], (ALLROWS, CHI), 1.0, 6.0, ((1, 8),)),
        "site_tensors": gaussian(key_of[1], (SITES, CHI, PHYS, CHI), CHI ** -0.5, 0.09375, ((0, 4), (3, 8))),
        "block_scales": jnp.clip(jnp.exp(math.log(1.0) - 1.3862944 * jax.random.uniform(key_of[2], (SITES, PHYS, CHI // BLOCK), jnp.float32) ** block_scale(key_of[2], (SITES, PHYS, CHI // BLOCK), ((0, 4), (2, 8)), -0.2, 0.2)), 0.25, 1.0),
        "displacement": gaussian(key_of[3], (SITES, PHYS, PHYS), 0.3, 0.9, ((0, 4),), jnp.float32),
        "outcomes": touch_ends(jax.random.randint(key_of[4], (SITES, ALLROWS), 0, PHYS), jax.random.fold_in(key_of[4], 1), 0, PHYS - 1).astype(jnp.int32),
    }


def reference(start_rows, site_tensors, block_scales, displacement, outcomes):
    entering = start_rows
    leaves = []
    logs = []
    for k in range(SITES):
        xf = entering.astype(jnp.float32)
        norm = jnp.sqrt(lax.optimization_barrier(jnp.mean(xf * xf, axis=1)) + 1e-06)
        logs.append(jnp.log(norm))
        prod = jnp.dot(entering, site_tensors[k].reshape(CHI, PHYS * CHI), preferred_element_type=jnp.float32)
        prod = prod.reshape(ALLROWS, PHYS, CHI // BLOCK, BLOCK) * block_scales[k][None, :, :, None]
        prod = prod.reshape(ALLROWS, PHYS, CHI)
        weight = displacement[k][outcomes[k]]
        mixed = jnp.einsum('bp,bpr->br', weight, prod)
        leave = (mixed / norm[:, None]).astype(jnp.bfloat16)
        leaves.append(leave)
        entering = leave
    return (jnp.stack(leaves), jnp.stack(logs))
```

```python
import functools
import jax
import jax.numpy as jnp
from jax import lax
from jax.experimental import pallas as pl
from jax.experimental.pallas import tpu as pltpu
from jax.sharding import PartitionSpec as P

ROWS = 128
CHUNK = 64
SLOTS = 4
LANES = 128
MESH = pl.DeviceIdType.MESH


def kernel(sites, bond, start_hbm, tensor_hbm, scale_ref, weight_ref, leave_ref, log_ref,
           mats, gathered, landing, wide, total,
           start_sem, load_sem, send_up, send_down, send_pair, send_site,
           recv_line, recv_pair, recv_site):
    chi, phys, cols = tensor_hbm.shape
    allrows = leave_ref.shape[0]
    rows = min(ROWS, allrows)
    batches = allrows // rows
    chips = bond // 2
    site = lax.axis_index("site")
    me = lax.axis_index("bond")
    chip = me // 2
    core = me % 2
    pair = me + 1 - 2 * core
    has_up = chip < chips - 1
    has_down = chip > 0
    first_site = site == 0
    has_next = site < sites - 1

    def block(ref, b, owner):
        return ref.at[pl.ds(pl.multiple_of(b * rows, rows), rows),
                      pl.ds(pl.multiple_of(owner * cols, cols), cols)]

    def up_copy(b, source):
        piece = block(gathered, b, 2 * source + core)
        return pltpu.make_async_remote_copy(
            piece, piece, send_up.at[b, source], recv_line.at[b, source],
            device_id={"bond": me + 2}, device_id_type=MESH)

    def down_copy(b, source):
        piece = block(gathered, b, 2 * source + core)
        return pltpu.make_async_remote_copy(
            piece, piece, send_down.at[b, source], recv_line.at[b, source],
            device_id={"bond": me - 2}, device_id_type=MESH)

    def pair_copy(b, source):
        piece = block(gathered, b, 2 * source + core)
        return pltpu.make_async_remote_copy(
            piece, piece, send_pair.at[b, source], recv_pair.at[b, source],
            device_id={"bond": pair}, device_id_type=MESH)

    def site_copy(b):
        return pltpu.make_async_remote_copy(
            leave_ref.at[pl.ds(pl.multiple_of(b * rows, rows), rows), :],
            block(gathered, b, me), send_site.at[b], recv_site.at[b],
            device_id={"site": site + 1}, device_id_type=MESH)

    def arrived_line(b, source):
        piece = block(gathered, b, 2 * source + core)
        pltpu.make_async_remote_copy(
            piece, piece, send_up.at[b, source], recv_line.at[b, source],
            device_id={"bond": pair}, device_id_type=MESH).wait_recv()

    def arrived_pair(b, source):
        piece = block(gathered, b, 2 * source + 1 - core)
        pltpu.make_async_remote_copy(
            piece, piece, send_pair.at[b, source], recv_pair.at[b, source],
            device_id={"bond": pair}, device_id_type=MESH).wait_recv()

    def relay(b, hop):
        if hop == 0:
            @pl.when(jnp.logical_not(first_site))
            def _():
                piece = block(gathered, b, me)
                pltpu.make_async_remote_copy(
                    piece, piece, send_site.at[b], recv_site.at[b],
                    device_id={"bond": pair}, device_id_type=MESH).wait_recv()

            @pl.when(has_up)
            def _():
                up_copy(b, chip).start()

            @pl.when(has_down)
            def _():
                down_copy(b, chip).start()

            pair_copy(b, chip).start()
            return

        @pl.when(chip - hop >= 0)
        def _():
            arrived_line(b, chip - hop)

            @pl.when(has_up)
            def _():
                up_copy(b, chip - hop).start()

            pair_copy(b, chip - hop).start()

        @pl.when(chip + hop < chips)
        def _():
            arrived_line(b, chip + hop)

            @pl.when(has_down)
            def _():
                down_copy(b, chip + hop).start()

            pair_copy(b, chip + hop).start()

    def load(step, slot):
        return pltpu.make_async_copy(
            tensor_hbm.at[pl.ds(pl.multiple_of(step * CHUNK, CHUNK), CHUNK)],
            landing.at[slot], load_sem.at[slot])

    steps = chi // CHUNK
    for step in range(SLOTS):
        load(step, step).start()

    @pl.when(first_site)
    def _():
        pltpu.make_async_copy(
            start_hbm, gathered.at[:, pl.ds(pl.multiple_of(me * cols, cols), cols)],
            start_sem).start()

    barrier = pltpu.get_barrier_semaphore()

    def greet(there, device):
        @pl.when(there)
        def _():
            pl.semaphore_signal(barrier, inc=1, device_id=device, device_id_type=MESH)

    around = ((has_up, {"bond": me + 2}), (has_down, {"bond": me - 2}),
              (chip >= 0, {"bond": pair}),
              (has_next, {"site": site + 1}), (site > 0, {"site": site - 1}))
    for there, device in around:
        greet(there, device)
    peers = sum(there.astype(jnp.int32) for there, _ in around)
    pl.semaphore_wait(barrier, peers)

    @pl.when(first_site)
    def _():
        pltpu.make_async_copy(
            start_hbm, gathered.at[:, pl.ds(pl.multiple_of(me * cols, cols), cols)],
            start_sem).wait()

    def spread(step, carry):
        slot = lax.rem(step, SLOTS)
        load(step, slot).wait()
        for t in range(cols // LANES):
            strip = slice(t * LANES, (t + 1) * LANES)
            wide[t] = landing[slot, :, :, strip].astype(jnp.float32).reshape(CHUNK * phys, LANES)
            for p in range(phys):
                mats[p, pl.ds(pl.multiple_of(step * CHUNK, CHUNK), CHUNK), strip] = (
                    wide[t, pl.ds(p, CHUNK, stride=phys), :].astype(jnp.bfloat16))

        @pl.when(step + SLOTS < steps)
        def _():
            load(step + SLOTS, slot).start()
        return carry

    for part in range(chips):
        @pl.when(first_site)
        def _():
            relay(0, part)
        lax.fori_loop(part * steps // chips, (part + 1) * steps // chips, spread, 0)

    @pl.when(jnp.logical_not(first_site))
    def _():
        for part in range(chips):
            relay(0, part)

    def batch(b, carry):
        for source in range(chips):
            arrived_pair(b, source)
        here = pl.ds(pl.multiple_of(b * rows, rows), rows)
        squares = jnp.zeros((rows, LANES), jnp.float32)
        for t in range(chi // LANES):
            x = gathered[here, t * LANES:(t + 1) * LANES].astype(jnp.float32)
            squares = squares + x * x
        norm = jnp.sqrt(jnp.sum(squares, axis=1, keepdims=True) / chi + 1e-06)
        log_ref[here, :] = jnp.log(norm)
        for p in range(phys):
            @pl.when(b + 1 < batches)
            def _():
                for part in range(p * chips // phys, (p + 1) * chips // phys):
                    relay(b + 1, part)
            prod = jnp.dot(gathered[here, :], mats[p], preferred_element_type=jnp.float32)
            prod = prod * scale_ref[p:p + 1, :] * weight_ref[here, p:p + 1]
            if p == 0:
                total[...] = prod
            elif p < phys - 1:
                total[...] += prod
            else:
                leave_ref[here, :] = ((total[...] + prod) / norm).astype(jnp.bfloat16)

        @pl.when(has_next)
        def _():
            site_copy(b).start()
        return carry

    lax.fori_loop(0, batches, batch, 0)

    def drain(b, carry):
        @pl.when(has_next)
        def _():
            site_copy(b).wait_send()
        for source in range(chips):
            pair_copy(b, source).wait_send()

            @pl.when(jnp.logical_and(has_up, source <= chip))
            def _():
                up_copy(b, source).wait_send()

            @pl.when(jnp.logical_and(has_down, source >= chip))
            def _():
                down_copy(b, source).wait_send()
        return carry

    lax.fori_loop(0, batches, drain, 0)


def local(start_rows, site_tensors, block_scales, displacement, outcomes):
    sites = lax.axis_size("site")
    bond = lax.axis_size("bond")
    _, chi, phys, cols = site_tensors.shape
    allrows = start_rows.shape[0]
    nblk = block_scales.shape[2]
    scales = jnp.repeat(block_scales[0], cols // nblk, axis=1)
    onehot = (outcomes[0][:, None] == jnp.arange(phys, dtype=jnp.int32)[None, :]).astype(jnp.float32)
    weight = jnp.sum(onehot[:, :, None] * displacement[0][None], axis=1)
    batches = allrows // min(ROWS, allrows)
    chips = bond // 2
    sems = pltpu.SemaphoreType.DMA
    leave, logs = pl.pallas_call(
        functools.partial(kernel, sites, bond),
        out_shape=(jax.ShapeDtypeStruct((allrows, cols), jnp.bfloat16),
                   jax.ShapeDtypeStruct((allrows, 1), jnp.float32)),
        in_specs=[pl.BlockSpec(memory_space=pl.ANY), pl.BlockSpec(memory_space=pl.ANY),
                  pl.BlockSpec(memory_space=pltpu.VMEM), pl.BlockSpec(memory_space=pltpu.VMEM)],
        out_specs=(pl.BlockSpec(memory_space=pltpu.VMEM), pl.BlockSpec(memory_space=pltpu.VMEM)),
        scratch_shapes=[
            pltpu.VMEM((phys, chi, cols), jnp.bfloat16),
            pltpu.VMEM((allrows, chi), jnp.bfloat16),
            pltpu.VMEM((SLOTS, CHUNK, phys, cols), jnp.bfloat16),
            pltpu.VMEM((cols // LANES, CHUNK * phys, LANES), jnp.float32),
            pltpu.VMEM((min(ROWS, allrows), cols), jnp.float32),
            sems(()), sems((SLOTS,)),
            sems((batches, chips)), sems((batches, chips)), sems((batches, chips)), sems((batches,)),
            sems((batches, chips)), sems((batches, chips)), sems((batches,)),
        ],
        compiler_params=pltpu.CompilerParams(
            collective_id=0, has_side_effects=True, vmem_limit_bytes=64000000),
    )(start_rows, site_tensors[0], scales, weight)
    return leave[None], logs[:, 0][None]


def solution(mesh):
    return jax.shard_map(
        local,
        mesh=mesh,
        in_specs=(
            P(None, "bond"),
            P("site", None, None, "bond"),
            P("site", None, "bond"),
            P("site", None, None),
            P("site", None),
        ),
        out_specs=(P("site", None, "bond"), P("site", None)),
        check_vma=False,
    )
```
